32 devices in a mesh: row: 4 (over y, x), col: 4 (over z), depth: 2 (over core).
Axes of the slice: x: 2, y: 2, z: 4, core: 2. Of those that a mesh axis runs over, the one named last changes fastest.
Arguments:
- features: bfloat16 [4096, 768], P(('row', 'col', 'depth')), may hold values from -6 to 6
- w_value: bfloat16 [768, 3072], replicated, may hold values from -0.21875 to 0.21875
- att_src: bfloat16 [4, 768], replicated, may hold values from -12 to 12
- att_dst: bfloat16 [4, 768], replicated, may hold values from -0.3984375 to 0.3984375
- tile_cols: int32 [32, 8], P('row'), may hold values from 0 to 31, as said below
- tile_count: int32 [32], P('row'), may hold values from 2 to 8, as said below
- neighbours: int32 [4096, 16], P('row'), may hold values from 0 to 4095, as said below
Outputs:
- mixed: bfloat16 [4096, 768], P(('row', 'col', 'depth'))
The draws below stay inside these ranges and needn't reach their ends.
Inputs may be any that keep to these rules, and one draw needn't show every extreme that they name: tile_cols[t, 0] is t itself and the 8 tiles of a row tile are distinct. Tile c lies in run c // 2 and in column group (c // 2) % 4. Of the 8 tiles of one row tile at most 2 lie in one column group, and some row tile lists 2 of one group among its first tile_count tiles. Every tile of row tile t lies in t's run or in one of the 7 runs that follow it, cyclically over 16 runs, and some listed tile lies in the last of these. `tile_count`: some row tile lists all 8. The 16 neighbours of node i are distinct, differ from i, and lie in tiles tile_cols[i // 128, s] with s < tile_count[i // 128].
All inputs are finite; a program needn't handle non-finite values.
Results may differ from the reference program's by a relative error of at most 0.0059.
Values may be sent and summed in bfloat16 or wider, within the bound.
No kernel may reach another device: no remote copies, remote signals or barrier semaphores. Data moves between devices by JAX's collectives and lax.ppermute only.
A program may use at most 64 MiB of HBM per device.

```python
import jax
import jax.numpy as jnp
from jax import lax

D = 768
HEADS = 4
TILE = 128
SLOTS = 8
KNN = 16
NTILES = 32
NODES = 4096
RUN = 2
COL_GROUPS = 4
RUNS = 16


def pattern(key):
    base_key = jax.random.fold_in(key, 4177)
    split_keys = jax.random.split(base_key, 8)
    tiles = jnp.arange(NTILES, dtype=jnp.int32)
    home_run = tiles // RUN
    forced = jax.random.randint(split_keys[0], (), 0, NTILES, dtype=jnp.int32)
    is_forced = tiles == forced
    rotation = jax.random.randint(split_keys[1], (NTILES,), 0, COL_GROUPS - 1, dtype=jnp.int32)
    rotation = jnp.where(is_forced, COL_GROUPS - 2, rotation)
    flipped = jax.random.randint(split_keys[2], (NTILES,), 0, 2, dtype=jnp.int32)
    flipped = jnp.where(is_forced, 1, flipped)
    extra_slots = jnp.arange(SLOTS - 2, dtype=jnp.int32)
    group_step = 1 + (extra_slots[None, :] + rotation[:, None]) % (COL_GROUPS - 1)
    second_lap = (extra_slots[None, :] // (COL_GROUPS - 1) + flipped[:, None]) % 2
    target_run = (home_run[:, None] + group_step + COL_GROUPS * second_lap) % RUNS
    within_run = jax.random.randint(split_keys[3], (NTILES, SLOTS - 2), 0, RUN, dtype=jnp.int32)
    others = target_run * RUN + within_run
    partner = jnp.bitwise_xor(tiles, 1)
    candidates = jnp.concatenate([partner[:, None], others], axis=1)
    order_score = jax.random.randint(split_keys[4], (NTILES, SLOTS - 1), 0, 1 << 20, dtype=jnp.int32) * SLOTS
    order_score = order_score + jnp.arange(SLOTS - 1, dtype=jnp.int32)[None, :]
    ordering = jnp.argsort(order_score, axis=1, stable=True)
    candidates = jnp.take_along_axis(candidates, ordering, axis=1)
    tile_table = jnp.concatenate([tiles[:, None], candidates], axis=1).astype(jnp.int32)
    counts = jax.random.randint(split_keys[5], (NTILES,), 2, SLOTS + 1, dtype=jnp.int32)
    counts = jnp.where(is_forced, SLOTS, counts).astype(jnp.int32)
    nodes = jnp.arange(NODES, dtype=jnp.int32)
    node_tile = nodes // TILE
    node_local = nodes % TILE
    node_count = counts[node_tile]
    nearest = jnp.arange(KNN, dtype=jnp.int32)
    slot_of = nearest[None, :] % node_count[:, None]
    lap_of = nearest[None, :] // node_count[:, None]
    stride = TILE // 8
    starting = jax.random.randint(split_keys[6], (NODES, SLOTS), 0, TILE, dtype=jnp.int32)
    jitter = jax.random.randint(split_keys[7], (NODES, KNN), 0, stride - 1, dtype=jnp.int32)
    spread = jnp.take_along_axis(starting, slot_of, axis=1) + stride * lap_of + jitter
    own_offset = (node_local[:, None] + 1 + spread % (TILE - 1)) % TILE
    other_offset = spread % TILE
    offset_in = jnp.where(slot_of == 0, own_offset, other_offset)
    column_tile = jnp.take_along_axis(tile_table[node_tile], slot_of, axis=1)
    near_ids = (column_tile * TILE + offset_in).astype(jnp.int32)
    return (tile_table, counts, near_ids)


def draw_tile_cols(key, part):
    return pattern(key)[0]


def draw_tile_count(key, part):
    return pattern(key)[1]


def draw_neighbours(key, part):
    return pattern(key)[2]


def draw_att_src(key, part):
    noise = jax.random.normal(jax.random.fold_in(key, 913), (HEADS, D), jnp.float32)
    return jnp.clip(0.05 * noise, -0.3, 0.3).astype(jnp.bfloat16)


def steps_of(stream_key, extent, shards, least, high):
    level = 1.0
    for axis_at, parts in shards:
        draws = jax.random.uniform(jax.random.fold_in(jax.random.fold_in(stream_key, 6), axis_at), (parts,), jnp.float32, least / len(shards), high / len(shards))
        level = level * jnp.repeat(jnp.exp(draws), extent[axis_at] // parts).reshape((-1,) + (1,) * (len(extent) - 1 - axis_at))
    return level


def normal_values(own_key, dims, width, limit, cuts=(), kind=jnp.bfloat16):
    entries = jax.random.normal(own_key, dims, jnp.float32) * width
    if len(cuts) > 0:
        entries = steps_of(own_key, dims, cuts, -0.22, 0.18) * entries
    return jnp.clip(entries, min=-limit, max=limit).astype(kind)


def setup_inputs(seed: int = 0) -> dict:
    splits = jax.random.split(jax.random.key(seed), 8)
    features = normal_values(splits[0], (NODES, D), 1.0, 6.0, ((0, 32),))
    w_value = normal_values(splits[1], (D, HEADS * D), D ** -0.5, 0.21875)
    att_src = draw_att_src(jax.random.fold_in(splits[7], 71), 0)
    att_dst = normal_values(splits[3], (HEADS, D), 0.08, 0.3984375)
    tile_cols = draw_tile_cols(jax.random.fold_in(splits[7], 71), 0)
    tile_count = draw_tile_count(jax.random.fold_in(splits[7], 71), 0)
    neighbours = draw_neighbours(jax.random.fold_in(splits[7], 71), 0)
    return dict(features=features, w_value=w_value, att_src=att_src, att_dst=att_dst, tile_cols=tile_cols, tile_count=tile_count, neighbours=neighbours)


LEAK_SLOPE = 0.2
NEG_BIG = -1.0e30


def leaky_relu(inputs):
    return jnp.where(inputs > 0, inputs, LEAK_SLOPE * inputs)


def head_scores(block_values, attention):
    shaped = block_values.reshape(block_values.shape[0], HEADS, D).astype(jnp.float32)
    return jnp.einsum("nhd,hd->nh", shaped, attention.astype(jnp.float32))


def reference(features, w_value, att_src, att_dst, tile_cols, tile_count, neighbours):
    value = jnp.dot(features, w_value, preferred_element_type=jnp.float32).astype(jnp.bfloat16)
    block_rows = 8 * TILE
    block_count = NODES // block_rows
    value_blocks = value.reshape(block_count, block_rows, HEADS * D)
    source_score = lax.map(lambda blocked: head_scores(blocked, att_src), value_blocks).reshape(NODES, HEADS)
    target_score = lax.map(lambda blocked: head_scores(blocked, att_dst), value_blocks).reshape(NODES, HEADS)
    slot_index = jnp.arange(SLOTS, dtype=jnp.int32)

    def one_block(block_index):
        block_start = (block_index * block_rows).astype(jnp.int32)
        node_ids = block_start + jnp.arange(block_rows, dtype=jnp.int32)
        near_ids = lax.dynamic_slice_in_dim(neighbours, block_start, block_rows, 0)
        home_tile = node_ids // TILE
        listed_tiles = tile_cols[home_tile]
        live_slots = slot_index[None, :] < tile_count[home_tile][:, None]
        near_tile = near_ids // TILE
        in_listed = jnp.any((listed_tiles[:, None, :] == near_tile[:, :, None]) & live_slots[:, None, :], axis=2)
        candidates = jnp.concatenate([node_ids[:, None], near_ids], axis=1)
        kept_mask = jnp.concatenate([jnp.ones((block_rows, 1), dtype=bool), in_listed], axis=1)
        logits = leaky_relu(source_score[node_ids][:, None, :] + target_score[candidates])
        logits = jnp.where(kept_mask[:, :, None], logits, NEG_BIG)
        row_peak = jnp.max(logits, axis=1, keepdims=True)
        weight = jnp.where(kept_mask[:, :, None], jnp.exp(logits - row_peak), 0.0)
        row_total = jnp.sum(weight, axis=1, keepdims=True)
        coefficient = (weight / row_total).astype(jnp.bfloat16)
        accumulated = jnp.zeros((block_rows, D), jnp.float32)
        for slot_number in range(KNN + 1):
            picked = value[candidates[:, slot_number]].reshape(block_rows, HEADS, D).astype(jnp.float32)
            accumulated = accumulated + jnp.einsum("nh,nhd->nd", coefficient[:, slot_number, :].astype(jnp.float32), picked)
        return jax.nn.elu(accumulated / HEADS).astype(jnp.bfloat16)

    mixed_blocks = lax.map(one_block, jnp.arange(block_count, dtype=jnp.int32))
    return mixed_blocks.reshape(NODES, D)
```

```python
import functools

import jax
import jax.numpy as jnp
from jax import lax
from jax.experimental import pallas as pl
from jax.experimental.pallas import tpu as pltpu
from jax.sharding import PartitionSpec as P

AXES = ("row", "col", "depth")
LEAK_SLOPE = 0.2
NEG_BIG = -1e30
VMEM = pltpu.VMEM
SMEM = pltpu.SMEM


def ahead(array, axis, by):
    length = lax.axis_size(axis)
    return lax.ppermute(array, axis, [((i + by) % length, i) for i in range(length)])


def score_kernel(features_ref, w_ref, src_ref, dst_ref, source_ref, target_ref):
    heads, width = src_ref.shape
    contract_last = (((1,), (1,)), ((), ()))
    for h in range(heads):
        value = jnp.dot(
            features_ref[...],
            w_ref[:, h * width : (h + 1) * width],
            preferred_element_type=jnp.float32,
        ).astype(jnp.bfloat16)
        source = lax.dot_general(
            value, src_ref[...], contract_last, preferred_element_type=jnp.float32
        )
        target = lax.dot_general(
            dst_ref[...], value, contract_last, preferred_element_type=jnp.float32
        )
        source_ref[:, h : h + 1] = source[:, h : h + 1]
        target_ref[h : h + 1, :] = target[h : h + 1, :]


def mask_kernel(chips, depths, tile, where_ref, cols_ref, count_ref, near_ref, mask_ref):
    rows, near_count = near_ref.shape
    own_tile, own_chip, own_depth = where_ref[0], where_ref[1], where_ref[2]
    near = near_ref[...]
    near_tile = near // tile
    kept = jnp.zeros(near.shape, jnp.bool_)
    for s in range(cols_ref.shape[1]):
        listed = jnp.where(s < count_ref[own_tile], cols_ref[own_tile, s], -1)
        kept = kept | (near_tile == listed)
    step = near_tile // depths - own_chip
    step = jnp.where(step < 0, step + chips, step)
    side = near_tile % depths - own_depth
    side = jnp.where(side < 0, side + depths, side)
    place = (step * depths + side) * tile + near % tile
    place = jnp.where(kept, place, -1)
    spot = lax.broadcasted_iota(jnp.int32, (rows, tile), 1)
    own = lax.broadcasted_iota(jnp.int32, (rows, tile), 0)
    for w in range(mask_ref.shape[1] // tile):
        linked = (spot == own) if w == 0 else None
        for k in range(near_count):
            hit = place[:, k : k + 1] - w * tile == spot
            linked = hit if linked is None else linked | hit
        mask_ref[:, w * tile : (w + 1) * tile] = jnp.where(linked, 0.0, NEG_BIG)


def coef_kernel(source_ref, target_ref, mask_ref, coef_ref):
    rows, _ = mask_ref.shape
    heads = source_ref.shape[1]
    block = 16
    for h in range(heads):

        def step(b, carry, h=h):
            at = pl.ds(pl.multiple_of(b * block, block), block)
            logits = source_ref[at, h : h + 1] + target_ref[h : h + 1, :]
            logits = jnp.maximum(logits, LEAK_SLOPE * logits) + mask_ref[at, :]
            peak = jnp.max(logits, axis=1, keepdims=True)
            weights = jnp.exp(logits - peak)
            total = jnp.sum(weights, axis=1, keepdims=True)
            out = pl.ds(pl.multiple_of(h * rows + b * block, block), block)
            coef_ref[out, :] = (weights * (1.0 / total)).astype(jnp.bfloat16)
            return carry

        lax.fori_loop(0, rows // block, step, 0)


def mix_kernel(tiles, coef_ref, w_ref, *refs):
    feature_refs, out_ref = refs[:tiles], refs[tiles]
    tile, width = feature_refs[0].shape
    rows = out_ref.shape[0]
    heads = coef_ref.shape[0] // rows
    gathered = None
    for i in range(tiles):
        part = jnp.dot(
            coef_ref[:, i * tile : (i + 1) * tile],
            feature_refs[i][...],
            preferred_element_type=jnp.float32,
        )
        gathered = part if gathered is None else gathered + part
    gathered = gathered.astype(jnp.bfloat16)
    total = None
    for h in range(heads):
        part = jnp.dot(
            gathered[h * rows : (h + 1) * rows],
            w_ref[:, h * width : (h + 1) * width],
            preferred_element_type=jnp.float32,
        )
        total = part if total is None else total + part
    mixed = total * (1.0 / heads)
    out_ref[...] = jnp.where(mixed > 0, mixed, jnp.exp(mixed) - 1.0).astype(out_ref.dtype)


def on_device(features, w_value, att_src, att_dst, tile_cols, tile_count, neighbours):
    rows, width = features.shape
    heads = att_src.shape[0]
    row_devices = lax.axis_size("row")
    col_devices = lax.axis_size("col")
    depths = lax.axis_size("depth")
    chips = row_devices * col_devices
    own_row = lax.axis_index("row")
    own_col = lax.axis_index("col")
    own_depth = lax.axis_index("depth")
    own_chip = own_row * col_devices + own_col
    tile = rows
    own_tile = own_col * depths + own_depth
    f32 = jnp.float32

    near_chips = [features] + [ahead(features, AXES, k * depths) for k in range(1, col_devices)]
    chip_features = near_chips + [ahead(x, "row", 1) for x in near_chips]
    window = []
    for x in chip_features:
        window.append(x)
        window.extend(ahead(x, "depth", d) for d in range(1, depths))
    tiles = len(window)

    vm, sm = pl.BlockSpec(memory_space=VMEM), pl.BlockSpec(memory_space=SMEM)
    source, target = pl.pallas_call(
        score_kernel,
        out_shape=(
            jax.ShapeDtypeStruct((rows, heads), f32),
            jax.ShapeDtypeStruct((heads, rows), f32),
        ),
        in_specs=[vm] * 4,
        out_specs=(vm, vm),
        cost_estimate=pl.CostEstimate(
            flops=2 * rows * w_value.size, bytes_accessed=2 * w_value.size, transcendentals=0
        ),
        name="scores",
    )(features, w_value, att_src, att_dst)

    own_near = lax.dynamic_slice_in_dim(neighbours, own_tile * tile, tile, 0)
    mask = pl.pallas_call(
        functools.partial(mask_kernel, chips, depths, tile),
        out_shape=jax.ShapeDtypeStruct((rows, tiles * tile), f32),
        in_specs=[sm, sm, sm, vm],
        out_specs=vm,
        cost_estimate=pl.CostEstimate(
            flops=4 * rows * tiles * tile * neighbours.shape[1],
            bytes_accessed=4 * rows * tiles * tile,
            transcendentals=0,
        ),
        name="mask",
    )(jnp.stack([own_tile, own_chip, own_depth]), tile_cols, tile_count, own_near)

    near_targets = [target] + [ahead(target, AXES, k * depths) for k in range(1, col_devices)]
    near_targets = jnp.stack(near_targets)
    side_targets = jnp.concatenate([near_targets, ahead(near_targets, "row", 1)])
    all_targets = jnp.stack([side_targets] + [ahead(side_targets, "depth", d) for d in range(1, depths)], axis=1)
    all_targets = jnp.transpose(all_targets, (2, 0, 1, 3)).reshape(heads, tiles * tile)

    coef = pl.pallas_call(
        coef_kernel,
        out_shape=jax.ShapeDtypeStruct((heads * rows, tiles * tile), jnp.bfloat16),
        in_specs=[vm] * 3,
        out_specs=vm,
        cost_estimate=pl.CostEstimate(
            flops=8 * heads * rows * tiles * tile,
            bytes_accessed=4 * heads * rows * tiles * tile,
            transcendentals=heads * rows * tiles * tile,
        ),
        name="coef",
    )(source, all_targets, mask)

    return pl.pallas_call(
        functools.partial(mix_kernel, tiles),
        out_shape=jax.ShapeDtypeStruct((rows, width), jnp.bfloat16),
        in_specs=[vm] * (2 + tiles),
        out_specs=vm,
        cost_estimate=pl.CostEstimate(
            flops=2 * heads * rows * width * (tiles * tile + width),
            bytes_accessed=2 * w_value.size,
            transcendentals=rows * width,
        ),
        name="mix",
    )(coef, w_value, *window)


def solution(mesh):
    placed = (
        P(AXES, None),
        P(),
        P(),
        P(),
        P("row", None),
        P("row"),
        P("row", None),
    )
    return jax.shard_map(
        on_device,
        mesh=mesh,
        in_specs=placed,
        out_specs=P(AXES, None),
        check_vma=False,
    )
```

```python
import functools

import jax
import jax.numpy as jnp
from jax import lax
from jax.experimental import pallas as pl
from jax.experimental.pallas import tpu as pltpu
from jax.sharding import PartitionSpec as P


AXES = ("row", "col", "depth")
LEAK_SLOPE = 0.2
NEG_BIG = -1e30
VM = pl.BlockSpec(memory_space=pltpu.VMEM)
SM = pl.BlockSpec(memory_space=pltpu.SMEM)
HBM = pl.BlockSpec(memory_space=pltpu.HBM)
ANY = pl.BlockSpec(memory_space=pl.ANY)
F32 = jnp.float32
BF16 = jnp.bfloat16


def ahead(array, axis, by):
    length = lax.axis_size(axis)
    return lax.ppermute(array, axis, [((i + by) % length, i) for i in range(length)])


def place_of_device():
    depths = lax.axis_size("depth")
    chip = lax.axis_index("row") * lax.axis_size("col") + lax.axis_index("col")
    depth = lax.axis_index("depth")
    return chip, depth, lax.axis_index("col") * depths + depth


def window_tile(tile, chip, depth, chips, depths):
    step = tile // depths - chip
    step = jnp.where(step < 0, step + chips, step)
    side = tile % depths - depth
    side = jnp.where(side < 0, side + depths, side)
    return step * depths + side


def slot_tiles(cols_ref, count_ref, chips, depths):
    chip, depth, own = place_of_device()
    count = count_ref[own]
    return [
        jnp.where(s < count, window_tile(cols_ref[own, s], chip, depth, chips, depths), 0)
        for s in range(cols_ref.shape[1])
    ], count


def score_kernel(features_ref, w_ref, src_ref, dst_ref, source_ref, target_ref):
    heads, width = src_ref.shape
    contract_last = (((1,), (1,)), ((), ()))
    for h in range(heads):
        value = jnp.dot(
            features_ref[...],
            w_ref[:, h * width : (h + 1) * width],
            preferred_element_type=F32,
        ).astype(BF16)
        source = lax.dot_general(value, src_ref[...], contract_last, preferred_element_type=F32)
        target = lax.dot_general(dst_ref[...], value, contract_last, preferred_element_type=F32)
        source_ref[:, h : h + 1] = source[:, h : h + 1]
        target_ref[h : h + 1, :] = target[h : h + 1, :]


def link_kernel(cols_ref, count_ref, near_ref, link_ref, near_scratch, sem):
    tile, near_count = near_scratch.shape
    _, _, own = place_of_device()
    copy = pltpu.make_async_copy(near_ref.at[pl.ds(own * tile, tile)], near_scratch, sem)
    copy.start()
    copy.wait()
    near = near_scratch[...]
    near_tile = near // tile
    bit = jnp.zeros(near.shape, jnp.int32)
    for s in range(cols_ref.shape[1]):
        listed = jnp.where(s < count_ref[own], cols_ref[own, s], -1)
        bit = jnp.where(near_tile == listed, 1 << s, bit)
    spot = near % tile
    lane = lax.broadcasted_iota(jnp.int32, (tile, tile), 1)
    row = lax.broadcasted_iota(jnp.int32, (tile, tile), 0)
    link = jnp.where(lane == row, 1, 0)
    for k in range(near_count):
        link = link | jnp.where(spot[:, k : k + 1] == lane, bit[:, k : k + 1], 0)
    link_ref[...] = link


def coef_kernel(chips, depths, cols_ref, count_ref, source_ref, link_ref, *refs):
    target_refs, (coef_ref, all_targets, targets) = refs[:-3], refs[-3:]
    steps, heads, tile = target_refs[0].shape
    for i, ref in enumerate(target_refs):
        part, side = i // depths, i % depths
        for k in range(steps):
            all_targets[(part * steps + k) * depths + side] = ref[k]
    places, _ = slot_tiles(cols_ref, count_ref, chips, depths)
    slots = len(places)
    for s in range(slots):
        targets[:, s * tile : (s + 1) * tile] = all_targets[places[s]]
    rows = source_ref.shape[0]
    block = 16

    def step(b, carry):
        at = pl.ds(pl.multiple_of(b * block, block), block)
        link = link_ref[at, :]
        linked = jnp.concatenate([link & (1 << s) for s in range(slots)], axis=1) != 0
        for h in range(heads):
            logits = source_ref[at, h : h + 1] + targets[h : h + 1, :]
            logits = jnp.where(linked, jnp.maximum(logits, LEAK_SLOPE * logits), NEG_BIG)
            peak = jnp.max(logits, axis=1, keepdims=True)
            weights = jnp.exp(logits - peak)
            total = jnp.sum(weights, axis=1, keepdims=True)
            out = pl.ds(pl.multiple_of(h * rows + b * block, block), block)
            coef_ref[out, :] = (weights * (1.0 / total)).astype(BF16)
        return carry

    lax.fori_loop(0, rows // block, step, 0)


def early_kernel(chips, depths, late, cols_ref, count_ref, coef_ref, *refs):
    feature_refs, (out_ref, picked, sems) = refs[:-3], refs[-3:]
    tile = feature_refs[0].shape[0]
    tiles = len(feature_refs) + late
    places, _ = slot_tiles(cols_ref, count_ref, chips, depths)
    for s, place in enumerate(places):
        at = picked.at[pl.ds(s * tile, tile)]

        @pl.when(place >= tiles - late)
        def _(at=at):
            at[...] = jnp.zeros(at.shape, at.dtype)

        for w, ref in enumerate(feature_refs):

            @pl.when(place == w)
            def _(ref=ref, at=at, s=s):
                pltpu.make_async_copy(ref, at, sems.at[s]).start()

    for s, place in enumerate(places):

        @pl.when(place < tiles - late)
        def _(s=s):
            at = picked.at[pl.ds(s * tile, tile)]
            pltpu.make_async_copy(feature_refs[0], at, sems.at[s]).wait()

    out_ref[...] = jnp.dot(coef_ref[...], picked[...], preferred_element_type=F32)


def late_kernel(chips, depths, cols_ref, count_ref, gathered_ref, coef_ref, w_ref, *refs):
    feature_refs, (out_ref, total_ref) = refs[:-2], refs[-2:]
    tile, width = feature_refs[0].shape
    rows = out_ref.shape[0]
    heads = coef_ref.shape[0] // rows
    tiles = 2 * lax.axis_size("col") * depths
    places, _ = slot_tiles(cols_ref, count_ref, chips, depths)
    total_ref[...] = gathered_ref[...]
    for s, place in enumerate(places):
        for w, ref in enumerate(feature_refs):

            @pl.when(place == tiles - len(feature_refs) + w)
            def _(ref=ref, s=s):
                total_ref[...] += jnp.dot(
                    coef_ref[:, s * tile : (s + 1) * tile], ref[...], preferred_element_type=F32
                )

    total = None
    for h in range(heads):
        part = jnp.dot(
            total_ref[h * rows : (h + 1) * rows].astype(BF16),
            w_ref[:, h * width : (h + 1) * width],
            preferred_element_type=F32,
        )
        total = part if total is None else total + part
    mixed = total * (1.0 / heads)
    out_ref[...] = jnp.where(mixed > 0, mixed, jnp.exp(mixed) - 1.0).astype(out_ref.dtype)


def scores_of(features, w_value, att_src, att_dst):
    rows, heads = features.shape[0], att_src.shape[0]
    return pl.pallas_call(
        score_kernel,
        out_shape=(
            jax.ShapeDtypeStruct((rows, heads), F32),
            jax.ShapeDtypeStruct((heads, rows), F32),
        ),
        in_specs=[VM] * 4,
        out_specs=(VM, VM),
        cost_estimate=pl.CostEstimate(
            flops=2 * rows * w_value.size, bytes_accessed=2 * w_value.size, transcendentals=0
        ),
        compiler_params=pltpu.CompilerParams(vmem_limit_bytes=16 << 20),
        name="scores",
    )(features, w_value, att_src, att_dst)


def links_of(tile_cols, tile_count, neighbours, tile):
    return pl.pallas_call(
        link_kernel,
        out_shape=jax.ShapeDtypeStruct((tile, tile), jnp.int32),
        in_specs=[SM, SM, HBM],
        out_specs=VM,
        scratch_shapes=[
            pltpu.VMEM((tile, neighbours.shape[1]), jnp.int32),
            pltpu.SemaphoreType.DMA,
        ],
        cost_estimate=pl.CostEstimate(
            flops=8 * tile * tile * neighbours.shape[1],
            bytes_accessed=4 * tile * tile,
            transcendentals=0,
        ),
        compiler_params=pltpu.CompilerParams(vmem_limit_bytes=4 << 20),
        name="links",
    )(tile_cols, tile_count, neighbours)


def coefs_of(chips, depths, tile_cols, tile_count, source, link, *targets):
    rows, heads = source.shape
    slots = tile_cols.shape[1]
    tile = link.shape[1]
    tiles = len(targets) * targets[0].shape[0]
    return pl.pallas_call(
        functools.partial(coef_kernel, chips, depths),
        out_shape=jax.ShapeDtypeStruct((heads * rows, slots * tile), BF16),
        in_specs=[SM, SM] + [VM] * (2 + len(targets)),
        out_specs=VM,
        scratch_shapes=[pltpu.VMEM((tiles, heads, tile), F32), pltpu.VMEM((heads, slots * tile), F32)],
        cost_estimate=pl.CostEstimate(
            flops=8 * heads * rows * slots * tile,
            bytes_accessed=4 * heads * rows * slots * tile,
            transcendentals=heads * rows * slots * tile,
        ),
        compiler_params=pltpu.CompilerParams(vmem_limit_bytes=8 << 20),
        name="coef",
    )(tile_cols, tile_count, source, link, *targets)


def early_of(chips, depths, late, tile_cols, tile_count, coef, *window):
    tile, width = window[0].shape
    slots = tile_cols.shape[1]
    return pl.pallas_call(
        functools.partial(early_kernel, chips, depths, late),
        out_shape=jax.ShapeDtypeStruct((coef.shape[0], width), F32),
        in_specs=[SM, SM, VM] + [ANY] * len(window),
        out_specs=VM,
        scratch_shapes=[pltpu.VMEM((slots * tile, width), BF16), pltpu.SemaphoreType.DMA((slots,))],
        cost_estimate=pl.CostEstimate(
            flops=2 * coef.size * width, bytes_accessed=6 * coef.size, transcendentals=0
        ),
        compiler_params=pltpu.CompilerParams(vmem_limit_bytes=12 << 20),
        name="early",
    )(tile_cols, tile_count, coef, *window)


def late_of(chips, depths, tile_cols, tile_count, gathered, coef, w_value, *window):
    tile, width = window[0].shape
    return pl.pallas_call(
        functools.partial(late_kernel, chips, depths),
        out_shape=jax.ShapeDtypeStruct((tile, width), BF16),
        in_specs=[SM, SM] + [VM] * (3 + len(window)),
        out_specs=VM,
        scratch_shapes=[pltpu.VMEM(gathered.shape, F32)],
        cost_estimate=pl.CostEstimate(
            flops=2 * tile * w_value.size, bytes_accessed=4 * gathered.size, transcendentals=tile * width
        ),
        compiler_params=pltpu.CompilerParams(vmem_limit_bytes=16 << 20),
        name="late",
    )(tile_cols, tile_count, gathered, coef, w_value, *window)


def on_device(features, w_value, att_src, att_dst, tile_cols, tile_count, neighbours):
    tile = features.shape[0]
    cols = lax.axis_size("col")
    depths = lax.axis_size("depth")
    chips = lax.axis_size("row") * cols
    cores = range(1, depths)

    near = [features] + [ahead(features, AXES, k * depths) for k in range(1, cols)]
    far = [ahead(x, "row", 1) for x in near]
    window = []
    for x in near + far:
        window += [x] + [ahead(x, "depth", d) for d in cores]

    source, target = scores_of(features, w_value, att_src, att_dst)
    link = links_of(tile_cols, tile_count, neighbours, tile)
    near_targets = [target] + [ahead(target, AXES, k * depths) for k in range(1, cols)]
    near_targets = jnp.stack(near_targets)
    targets = []
    for t in (near_targets, ahead(near_targets, "row", 1)):
        targets += [t] + [ahead(t, "depth", d) for d in cores]

    coef = coefs_of(chips, depths, tile_cols, tile_count, source, link, *targets)
    gathered = early_of(chips, depths, depths, tile_cols, tile_count, coef, *window[:-depths])
    return late_of(chips, depths, tile_cols, tile_count, gathered, coef, w_value, *window[-depths:])


def solution(mesh):
    placed = (
        P(AXES, None),
        P(),
        P(),
        P(),
        P("row", None),
        P("row"),
        P("row", None),
    )

    return jax.shard_map(
        on_device,
        mesh=mesh,
        in_specs=placed,
        out_specs=P(AXES, None),
        check_vma=False,
    )
```

```python
import functools

import jax
import jax.numpy as jnp
from jax import lax
from jax.experimental import pallas as pl
from jax.experimental.pallas import tpu as pltpu
from jax.sharding import PartitionSpec as P


AXES = ("row", "col", "depth")
LEAK_SLOPE = 0.2
NEG_BIG = -1e30
VM = pl.BlockSpec(memory_space=pltpu.VMEM)
SM = pl.BlockSpec(memory_space=pltpu.SMEM)
HBM = pl.BlockSpec(memory_space=pltpu.HBM)
ANY = pl.BlockSpec(memory_space=pl.ANY)
F32 = jnp.float32
BF16 = jnp.bfloat16

EXTRA = 8

LAST = (((1,), (1,)), ((), ()))


def ahead(array, axis, by):
    length = lax.axis_size(axis)
    return lax.ppermute(array, axis, [((i + by) % length, i) for i in range(length)])


def place_of_device():
    depths = lax.axis_size("depth")
    chip = lax.axis_index("row") * lax.axis_size("col") + lax.axis_index("col")
    depth = lax.axis_index("depth")
    return chip, depth, lax.axis_index("col") * depths + depth


def window_tile(tile, chip, depth, chips, depths):
    step = tile // depths - chip
    step = jnp.where(step < 0, step + chips, step)
    side = tile % depths - depth
    side = jnp.where(side < 0, side + depths, side)
    return step * depths + side


def slot_tiles(cols_ref, count_ref, chips, depths):
    chip, depth, own = place_of_device()
    count = count_ref[own]
    return [
        jnp.where(s < count, window_tile(cols_ref[own, s], chip, depth, chips, depths), 0)
        for s in range(cols_ref.shape[1])
    ], count


def put_scores(message_ref, head, scores):
    rows = scores.shape[1]
    parts, rest = [], scores
    for _ in range(3):
        part = rest.astype(BF16).astype(F32)
        rest = rest - part
        parts.append(part)
    parts.append(jnp.zeros((EXTRA - 3, rows), F32))
    message_ref[rows:, head * rows : (head + 1) * rows] = jnp.concatenate(parts, axis=0).astype(BF16)


def score_kernel(features_ref, w_ref, src_ref, dst_ref, source_ref, message_ref, x, src, dst, w, sems):
    rows, _ = features_ref.shape
    heads, width = src_ref.shape
    small = [
        pltpu.make_async_copy(a, b, sems.at[heads + i])
        for i, (a, b) in enumerate(((features_ref, x), (src_ref, src), (dst_ref, dst)))
    ]
    copies = [
        pltpu.make_async_copy(w_ref.at[:, pl.ds(h * width, width)], w.at[h], sems.at[h])
        for h in range(heads)
    ]
    for copy in small + copies:
        copy.start()
    for copy in small:
        copy.wait()
    message_ref[:rows] = x[...]
    message_ref[rows:] = jnp.zeros((EXTRA, message_ref.shape[1]), BF16)
    for h in range(heads):
        copies[h].wait()
        value = jnp.dot(x[...], w[h], preferred_element_type=F32).astype(BF16)
        source = lax.dot_general(value, src[...], LAST, preferred_element_type=F32)
        target = lax.dot_general(dst[...], value, LAST, preferred_element_type=F32)
        source_ref[:, h : h + 1] = source[:, h : h + 1]
        put_scores(message_ref, h, target[h : h + 1, :])


def message_kernel(features_ref, w_ref, dst_ref, message_ref):
    rows, _ = features_ref.shape
    heads, width = dst_ref.shape
    message_ref[:rows] = features_ref[...]
    message_ref[rows:] = jnp.zeros((EXTRA, message_ref.shape[1]), BF16)
    for h in range(heads):
        value = jnp.dot(
            features_ref[...], w_ref[:, h * width : (h + 1) * width], preferred_element_type=F32
        ).astype(BF16)
        target = lax.dot_general(dst_ref[...], value, LAST, preferred_element_type=F32)
        put_scores(message_ref, h, target[h : h + 1, :])


def link_kernel(cols_ref, count_ref, near_ref, link_ref, near_scratch, sem):
    tile, near_count = near_scratch.shape
    _, _, own = place_of_device()
    copy = pltpu.make_async_copy(near_ref.at[pl.ds(own * tile, tile)], near_scratch, sem)
    copy.start()
    copy.wait()
    near = near_scratch[...]
    near_tile = near // tile
    bit = jnp.zeros(near.shape, jnp.int32)
    for s in range(cols_ref.shape[1]):
        listed = jnp.where(s < count_ref[own], cols_ref[own, s], -1)
        bit = jnp.where(near_tile == listed, 1 << s, bit)
    spot = near % tile
    lane = lax.broadcasted_iota(jnp.int32, (tile, tile), 1)
    row = lax.broadcasted_iota(jnp.int32, (tile, tile), 0)
    link = jnp.where(lane == row, 1, 0)
    for k in range(near_count):
        link = link | jnp.where(spot[:, k : k + 1] == lane, bit[:, k : k + 1], 0)
    link_ref[...] = link


def slot_of(window_place, places, listed):
    slot = -1
    for s, place in enumerate(places):
        slot = jnp.where((place == window_place) & listed[s], s, slot)
    return slot


def scores_in(extra, head, tile):
    parts = extra[:, head * tile : (head + 1) * tile].astype(F32)
    return parts[0:1] + parts[1:2] + parts[2:3]


def first_kernel(chips, depths, cols_ref, count_ref, source_ref, link_ref, *refs):
    message_refs, refs = refs[:-8], refs[-8:]
    peak_ref, total_ref, mixed_ref, picked, extras, targets, coef, sems = refs
    tile, heads = source_ref.shape
    places, count = slot_tiles(cols_ref, count_ref, chips, depths)
    slots = len(places)
    listed = [s < count for s in range(slots)]
    for w, ref in enumerate(message_refs):
        slot = slot_of(w, places, listed)

        @pl.when(slot >= 0)
        def _(ref=ref, slot=slot):
            pltpu.make_async_copy(
                ref.at[pl.ds(tile, EXTRA)], extras.at[slot], sems.at[0, slot]
            ).start()
            at = picked.at[pl.ds(pl.multiple_of(slot * tile, tile), tile)]
            pltpu.make_async_copy(ref.at[pl.ds(0, tile)], at, sems.at[1, slot]).start()

    held = 0
    copied = [listed[s] & (places[s] < len(message_refs)) for s in range(slots)]
    for s in range(slots):
        held = held + jnp.where(copied[s], 1 << s, 0)

        @pl.when(copied[s])
        def _(s=s):
            pltpu.make_async_copy(
                message_refs[0].at[pl.ds(tile, EXTRA)], extras.at[s], sems.at[0, s]
            ).wait()

        for h in range(heads):
            targets[h : h + 1, s * tile : (s + 1) * tile] = scores_in(extras[s], h, tile)

    block = 16

    def step(b, carry):
        at = pl.ds(pl.multiple_of(b * block, block), block)
        link = link_ref[at, :] & held
        linked = jnp.concatenate([link & (1 << s) for s in range(slots)], axis=1) != 0
        for h in range(heads):
            logits = source_ref[at, h : h + 1] + targets[h : h + 1, :]
            logits = jnp.where(linked, jnp.maximum(logits, LEAK_SLOPE * logits), NEG_BIG)
            peak = jnp.max(logits, axis=1, keepdims=True)
            weights = jnp.exp(logits - peak)
            peak_ref[at, h : h + 1] = peak
            total_ref[at, h : h + 1] = jnp.sum(weights, axis=1, keepdims=True)
            out = pl.ds(pl.multiple_of(h * tile + b * block, block), block)
            coef[out, :] = weights.astype(BF16)
        return carry

    lax.fori_loop(0, tile // block, step, 0)

    for s in range(slots):
        at = picked.at[pl.ds(s * tile, tile)]

        @pl.when(copied[s])
        def _(at=at, s=s):
            pltpu.make_async_copy(message_refs[0].at[pl.ds(0, tile)], at, sems.at[1, s]).wait()

        @pl.when(jnp.logical_not(copied[s]))
        def _(at=at):
            at[...] = jnp.zeros(at.shape, at.dtype)

    mixed_ref[...] = jnp.dot(coef[...], picked[...], preferred_element_type=F32)


def next_kernel(chips, depths, first, last, cols_ref, count_ref, source_ref, link_ref, *refs):
    tile, heads = source_ref.shape
    peak_in, total_in, mixed_in = refs[:3]
    if last:
        w_ref, message_refs = refs[3], refs[4:-3]
        out_ref, targets, coef = refs[-3:]
    else:
        message_refs = refs[3:-5]
        peak_ref, total_ref, mixed_ref, targets, coef = refs[-5:]
    width = mixed_in.shape[1]
    places, count = slot_tiles(cols_ref, count_ref, chips, depths)
    listed = [s < count for s in range(len(places))]
    bits = []
    for i, ref in enumerate(message_refs):
        slot = slot_of(first + i, places, listed)
        bits.append(jnp.where(slot >= 0, jnp.left_shift(1, jnp.maximum(slot, 0)), 0))
        for h in range(heads):
            targets[h : h + 1, i * tile : (i + 1) * tile] = scores_in(ref[tile:, :], h, tile)
    link = link_ref[...]
    linked = jnp.concatenate([link & bit for bit in bits], axis=1) != 0
    features = jnp.concatenate([ref[:tile, :] for ref in message_refs], axis=0)
    total = None
    for h in range(heads):
        logits = source_ref[:, h : h + 1] + targets[h : h + 1, :]
        logits = jnp.where(linked, jnp.maximum(logits, LEAK_SLOPE * logits), NEG_BIG)
        before = peak_in[:, h : h + 1]
        peak = jnp.maximum(before, jnp.max(logits, axis=1, keepdims=True))
        fade = jnp.exp(before - peak)
        weights = jnp.exp(logits - peak)
        weight = total_in[:, h : h + 1] * fade + jnp.sum(weights, axis=1, keepdims=True)
        weights = weights.astype(BF16)
        mixed = mixed_in[h * tile : (h + 1) * tile, :] * fade
        mixed = mixed + jnp.dot(weights, features, preferred_element_type=F32)
        if last:
            part = jnp.dot(
                (mixed * (1.0 / weight)).astype(BF16),
                w_ref[:, h * width : (h + 1) * width],
                preferred_element_type=F32,
            )
            total = part if total is None else total + part
        else:
            peak_ref[:, h : h + 1] = peak
            total_ref[:, h : h + 1] = weight
            mixed_ref[h * tile : (h + 1) * tile, :] = mixed
    if last:
        out = total * (1.0 / heads)
        out_ref[...] = jnp.where(out > 0, out, jnp.exp(out) - 1.0).astype(out_ref.dtype)


def scores_of(features, w_value, att_src, att_dst):
    (rows, width), heads = features.shape, att_src.shape[0]
    inputs = (features, w_value, att_src, att_dst)
    return pl.pallas_call(
        score_kernel,
        out_shape=(
            jax.ShapeDtypeStruct((rows, heads), F32),
            jax.ShapeDtypeStruct((rows + EXTRA, width), BF16),
        ),
        in_specs=[HBM] * 4,
        out_specs=(VM, VM),
        scratch_shapes=[
            pltpu.VMEM(features.shape, BF16),
            pltpu.VMEM(att_src.shape, BF16),
            pltpu.VMEM(att_dst.shape, BF16),
            pltpu.VMEM((heads, w_value.shape[0], att_src.shape[1]), BF16),
            pltpu.SemaphoreType.DMA((heads + 3,)),
        ],
        cost_estimate=pl.CostEstimate(
            flops=rows, bytes_accessed=rows, transcendentals=0
        ),
        compiler_params=pltpu.CompilerParams(vmem_limit_bytes=16 << 20),
        name="scores",
    )(*[pltpu.with_memory_space_constraint(x, pltpu.HBM) for x in inputs])


def message_of(features, w_value, att_dst):
    (rows, width) = features.shape
    return pl.pallas_call(
        message_kernel,
        out_shape=jax.ShapeDtypeStruct((rows + EXTRA, width), BF16),
        in_specs=[VM] * 3,
        out_specs=VM,
        cost_estimate=pl.CostEstimate(
            flops=2 * rows * w_value.size, bytes_accessed=2 * w_value.size, transcendentals=0
        ),
        compiler_params=pltpu.CompilerParams(vmem_limit_bytes=8 << 20),
        name="message",
    )(features, w_value, att_dst)


def links_of(tile_cols, tile_count, neighbours, tile):
    return pl.pallas_call(
        link_kernel,
        out_shape=jax.ShapeDtypeStruct((tile, tile), jnp.int32),
        in_specs=[SM, SM, HBM],
        out_specs=VM,
        scratch_shapes=[
            pltpu.VMEM((tile, neighbours.shape[1]), jnp.int32),
            pltpu.SemaphoreType.DMA,
        ],
        cost_estimate=pl.CostEstimate(
            flops=tile, bytes_accessed=tile, transcendentals=0
        ),
        compiler_params=pltpu.CompilerParams(vmem_limit_bytes=4 << 20),
        name="links",
    )(tile_cols, tile_count, neighbours)


def stats_shape(tile, heads, width):
    return (
        jax.ShapeDtypeStruct((tile, heads), F32),
        jax.ShapeDtypeStruct((tile, heads), F32),
        jax.ShapeDtypeStruct((heads * tile, width), F32),
    )


def first_of(chips, depths, tile_cols, tile_count, source, link, *messages):
    tile, heads = source.shape
    width = messages[0].shape[1]
    slots = tile_cols.shape[1]
    return pl.pallas_call(
        functools.partial(first_kernel, chips, depths),
        out_shape=stats_shape(tile, heads, width),
        in_specs=[SM, SM, VM, VM] + [ANY] * len(messages),
        out_specs=(VM,) * 3,
        scratch_shapes=[
            pltpu.VMEM((slots * tile, width), BF16),
            pltpu.VMEM((slots, EXTRA, width), BF16),
            pltpu.VMEM((heads, slots * tile), F32),
            pltpu.VMEM((heads * tile, slots * tile), BF16),
            pltpu.SemaphoreType.DMA((2, slots)),
        ],
        cost_estimate=pl.CostEstimate(
            flops=2 * heads * tile * slots * tile * width,
            bytes_accessed=8 * heads * tile * width,
            transcendentals=heads * tile * slots * tile,
        ),
        compiler_params=pltpu.CompilerParams(vmem_limit_bytes=14 << 20),
        name="first",
    )(tile_cols, tile_count, source, link, *messages)


def next_of(chips, depths, first, tile_cols, tile_count, source, link, state, w_value, *messages):
    tile, heads = source.shape
    width = messages[0].shape[1]
    last = w_value is not None
    return pl.pallas_call(
        functools.partial(next_kernel, chips, depths, first, last),
        out_shape=jax.ShapeDtypeStruct((tile, width), BF16) if last else stats_shape(tile, heads, width),
        in_specs=[SM, SM] + [VM] * (5 + last + len(messages)),
        out_specs=VM if last else (VM,) * 3,
        scratch_shapes=[
            pltpu.VMEM((heads, len(messages) * tile), F32),
            pltpu.VMEM((heads * tile, len(messages) * tile), BF16),
        ],
        cost_estimate=pl.CostEstimate(
            flops=2 * heads * tile * tile * width * (len(messages) + 6 * last),
            bytes_accessed=8 * heads * tile * width,
            transcendentals=heads * tile * tile * len(messages),
        ),
        compiler_params=pltpu.CompilerParams(vmem_limit_bytes=14 << 20),
        name="final" if last else "middle",
    )(tile_cols, tile_count, source, link, *state, *((w_value,) if last else ()), *messages)


def on_device(features, w_value, att_src, att_dst, tile_cols, tile_count, neighbours):
    tile = features.shape[0]
    cols = lax.axis_size("col")
    depths = lax.axis_size("depth")
    chips = lax.axis_size("row") * cols
    cores = range(1, depths)

    source, message = scores_of(features, w_value, att_src, att_dst)
    link = links_of(tile_cols, tile_count, neighbours, tile)

    near = [message]
    for k in range(1, cols):
        arrived = ahead(features, AXES, k * depths)
        near.append(message_of(arrived, w_value, att_dst))
    far = [ahead(x, "row", 1) for x in near]
    window = []
    for x in near + far:
        window += [x] + [ahead(x, "depth", d) for d in cores]

    common = (tile_cols, tile_count, source, link)
    a, b = (cols + 1) * depths, len(window) - depths
    state = first_of(chips, depths, *common, *window[:a])
    state = next_of(chips, depths, a, *common, state, None, *window[a:b])
    return next_of(chips, depths, b, *common, state, w_value, *window[b:])


def solution(mesh):
    placed = (
        P(AXES, None),
        P(),
        P(),
        P(),
        P("row", None),
        P("row"),
        P("row", None),
    )

    return jax.shard_map(
        on_device,
        mesh=mesh,
        in_specs=placed,
        out_specs=P(AXES, None),
        check_vma=False,
    )
```
